32 devices in a mesh: row: 8 (over z, core), col: 4 (over y, x).
Axes of the slice: x: 2, y: 2, z: 4, core: 2. Of those that a mesh axis runs over, the one named last changes fastest.
Arguments:
- solved: float32 [2, 8192, 512], P(None, 'row'), may hold values from -6 to 6
- upper_cols: float32 [2, 2, 1024, 8192], P(None, None, 'col', 'row'), may hold values from -0.046875 to 0.046875
- coupling: float32 [2, 1024, 1024], P(None, 'col', 'row'), may hold values from -0.125 to 0.125
- inverse_diag: float32 [2, 2, 1024, 1024], P(None, None, 'row', 'col'), may hold values from -0.1875 to 0.1875
- right_side: float32 [2, 2, 1024, 512], P(None, None, 'col'), may hold values from -6 to 6
Outputs:
- answers: float32 [2, 2, 1024, 512], P(None, None, 'row')
The draws below stay inside these ranges and needn't reach their ends.
All inputs are finite; a program needn't handle non-finite values.
Results may differ from the reference program's by a relative error of at most 0.000082.
Values sent between devices are 32-bit elements; how exact they have to be, the bound alone decides.
No kernel may reach another device: no remote copies, remote signals or barrier semaphores. Data moves between devices by JAX's collectives and lax.ppermute only.
A program may use at most 64 MiB of HBM per device.

```python
import jax
import jax.numpy as jnp
from jax import lax

PANEL = 1024
NRHS = 512
SOLVED = 8192


def levels(rng, dims, shards, low, top_value):
    factor_of = 1.0
    for position, shards_of in shards:
        heights = jax.random.uniform(jax.random.fold_in(jax.random.fold_in(rng, 6), position), (shards_of,), jnp.float32, low / len(shards), top_value / len(shards))
        factor_of = factor_of * jnp.repeat(jnp.exp(heights), dims[position] // shards_of).reshape((-1,) + (1,) * (len(dims) - 1 - position))
    return factor_of


def normal_values(own_key, shape, scale, reach, shards=(), kind=jnp.bfloat16):
    array = jax.random.normal(own_key, shape, jnp.float32) * scale
    if len(shards) > 0:
        array = levels(own_key, shape, shards, -0.22, 0.18) * array
    return jnp.clip(array, min=-reach, max=reach).astype(kind)


def setup_inputs(seed: int = 0) -> dict:
    streams_of = jax.random.split(jax.random.key(seed), 6)
    solved = normal_values(streams_of[0], (2, SOLVED, NRHS), 1.0, 6.0, ((1, 8),), jnp.float32)
    upper_cols = normal_values(streams_of[1], (2, 2, PANEL, SOLVED), (2 * SOLVED) ** -0.5, 0.046875, ((2, 4), (3, 8)), jnp.float32)
    coupling = normal_values(streams_of[2], (2, PANEL, PANEL), (2 * PANEL) ** -0.5, 0.125, ((1, 4), (2, 8)), jnp.float32)
    inverse_diag = normal_values(streams_of[3], (2, 2, PANEL, PANEL), PANEL ** -0.5, 0.1875, ((2, 8), (3, 4)), jnp.float32)
    right_side = normal_values(streams_of[4], (2, 2, PANEL, NRHS), 1.0, 6.0, ((2, 4),), jnp.float32)
    return dict(solved=solved, upper_cols=upper_cols, coupling=coupling, inverse_diag=inverse_diag, right_side=right_side)


HIGHEST = lax.Precision.HIGHEST


def conj_apply(factor, vector):
    parts = jnp.einsum("smk,tkn->stmn", factor, vector, precision=HIGHEST)
    return jnp.stack([parts[0, 0] + parts[1, 1], parts[0, 1] - parts[1, 0]])


def complex_apply(matrix, vector):
    parts = jnp.einsum("smk,tkn->stmn", matrix, vector, precision=HIGHEST)
    return jnp.stack([parts[0, 0] - parts[1, 1], parts[0, 1] + parts[1, 0]])


def reference(solved, upper_cols, coupling, inverse_diag, right_side):
    prior_first = conj_apply(upper_cols[:, 0], solved)
    prior_second = conj_apply(upper_cols[:, 1], solved)
    answer_first = complex_apply(jnp.tril(inverse_diag[:, 0]), right_side[:, 0] - prior_first)
    coupled = conj_apply(coupling, answer_first)
    answer_second = complex_apply(jnp.tril(inverse_diag[:, 1]), right_side[:, 1] - (prior_second + coupled))
    return jnp.stack([answer_first, answer_second], axis=1)
```

```python
import jax
import jax.numpy as jnp
from jax import lax
from jax.sharding import PartitionSpec as P

PRECISION = lax.Precision.HIGH

CORE = 1
NEAR = 2
SIDE = 1


def conj_apply(factor, vector):
    parts = jnp.einsum("smk,tkn->stmn", factor, vector, precision=PRECISION)
    return jnp.stack([parts[0, 0] + parts[1, 1], parts[0, 1] - parts[1, 0]])


def complex_apply(matrix, vector):
    parts = jnp.einsum("smk,tkn->stmn", matrix, vector, precision=PRECISION)
    return jnp.stack([parts[0, 0] - parts[1, 1], parts[0, 1] + parts[1, 0]])


def solution(mesh):
    n_row, n_col = mesh.shape["row"], mesh.shape["col"]

    def swap(value, axis, bit):
        size = mesh.shape[axis]
        return lax.ppermute(value, axis, [(i, i ^ bit) for i in range(size)])

    def sum_over(value, axis, first_bit):
        bit = first_bit
        while bit < mesh.shape[axis]:
            value = value + swap(value, axis, bit)
            bit *= 2
        return value

    def ordered(mine, other, flag, axis):
        low = jnp.where(flag == 0, mine, other)
        high = jnp.where(flag == 0, other, mine)
        return jnp.concatenate([low, high], axis=axis)

    def per_device(solved, upper_cols, coupling, inverse_diag, right_side):
        row, col = lax.axis_index("row"), lax.axis_index("col")
        core, near, side = row & 1, (row >> 1) & 1, col & 1
        far_first = (row >> 2) == 0
        rows, cols = inverse_diag.shape[2], inverse_diag.shape[3]
        half = cols // 2
        quarter = right_side.shape[3] // 4

        row_ids = row * rows + jnp.arange(rows, dtype=jnp.int32)
        col_ids = col * cols + jnp.arange(cols, dtype=jnp.int32)
        inverse = jnp.where(col_ids[None, :] <= row_ids[:, None], inverse_diag, 0.0)

        def gather_matrix(block, near_axis, side_axis):
            block = jnp.concatenate([block, swap(block, "row", NEAR)], axis=near_axis)
            return jnp.concatenate([block, swap(block, "col", SIDE)], axis=side_axis)

        def prior(panel):
            factor = upper_cols[:, panel]
            mine = lax.dynamic_slice_in_dim(factor, core * half, half, axis=1)
            other = lax.dynamic_slice_in_dim(factor, (1 - core) * half, half, axis=1)
            given = swap(conj_apply(other, solved), "row", CORE)
            value = conj_apply(mine, solved) + given
            value = value.reshape(2, half, 2, 2 * quarter)
            keep = lax.dynamic_index_in_dim(value, near, 2, keepdims=False)
            send = lax.dynamic_index_in_dim(value, 1 - near, 2, keepdims=False)
            value = keep + swap(send, "row", NEAR)
            right = lax.dynamic_slice(
                right_side[:, panel], (0, core * half, near * 2 * quarter), (2, half, 2 * quarter)
            )
            value = jnp.where(far_first, right, 0.0) - value
            value = value.reshape(2, half, 2, quarter)
            keep = lax.dynamic_index_in_dim(value, side, 2, keepdims=False)
            send = lax.dynamic_index_in_dim(value, 1 - side, 2, keepdims=False)
            return jnp.stack([keep, swap(send, "col", SIDE)], axis=1)

        def complete(value):
            value = sum_over(value, "row", 2 * NEAR)
            other = swap(value, "row", CORE)
            value = ordered(value[:, :, None], other[:, :, None], core, 2)
            return value.reshape(2, 2 * cols, quarter)

        def spread(answer):
            mine, other = answer[:, :rows], answer[:, rows:]
            got = swap(other, "row", NEAR)
            mine = ordered(mine[:, :, None], got[:, :, None], near, 2)
            got = swap(mine, "col", SIDE)
            whole = ordered(mine[:, :, :, None], got[:, :, :, None], side, 3)
            return whole.reshape(2, rows, 4 * quarter)

        first_inverse = gather_matrix(inverse[:, 0], 1, 2)
        first = complete(prior(0))
        answer_first = sum_over(complex_apply(first_inverse, first), "col", 2 * SIDE)
        couple = gather_matrix(coupling, 2, 1)
        coupled = conj_apply(couple, answer_first).reshape(2, 2, 2, half, quarter)
        keep = lax.dynamic_index_in_dim(coupled, core, 2, keepdims=False)
        send = lax.dynamic_index_in_dim(coupled, 1 - core, 2, keepdims=False)
        coupled = keep + swap(send, "row", CORE)
        second_inverse = gather_matrix(inverse[:, 1], 1, 2)
        second = complete(prior(1) - coupled)
        answer_second = sum_over(complex_apply(second_inverse, second), "col", 2 * SIDE)
        return jnp.stack([spread(answer_first), spread(answer_second)], axis=1)

    in_specs = (
        P(None, "row", None),
        P(None, None, "col", "row"),
        P(None, "col", "row"),
        P(None, None, "row", "col"),
        P(None, None, "col", None),
    )
    return jax.shard_map(
        per_device, mesh=mesh, in_specs=in_specs, out_specs=P(None, None, "row", None), check_vma=False
    )
```

```python
import functools

import jax
import jax.numpy as jnp
from jax import lax
from jax.experimental import pallas as pl
from jax.experimental.pallas import tpu as pltpu
from jax.sharding import PartitionSpec as P

CORE = 1
NEAR = 2
SIDE = 1
F32 = jnp.float32
BF16 = jnp.bfloat16
MIB = 1 << 20


def split(value):
    high = value.astype(BF16)
    return high, (value - high.astype(F32)).astype(BF16)


def dot(left, right):
    return jnp.dot(left, right, preferred_element_type=F32)


def product(left, right):
    (high, low), (both, right_high) = left, right
    width = right_high.shape[1]
    full = dot(high, both)
    return full[:, :width] + (full[:, width:] + dot(low, right_high))


def packed_right(value):
    high, low = split(value)
    return jnp.concatenate([high, low], axis=1), high


def lane_is_low(shape):
    return lax.broadcasted_iota(jnp.int32, shape, 1) < shape[1] // 2


def swap_halves(value):
    return pltpu.roll(value, value.shape[1] // 2, 1)


def complex_product(real, imag, right, conj):
    plain = product(split(real), right)
    cross = swap_halves(product(split(imag), right))
    low = lane_is_low(plain.shape)
    return plain + jnp.where(low if conj else jnp.logical_not(low), cross, -cross)


def call(kernel, ids, arrays, outs, vmem=12 * MIB, flops=0):
    moved = sum(a.size * 4 for a in arrays) + sum(4 * o.size for o in outs)
    return pl.pallas_call(
        kernel,
        out_shape=outs,
        in_specs=[pl.BlockSpec(memory_space=pltpu.SMEM)] + [pl.BlockSpec(memory_space=pltpu.VMEM)] * len(arrays),
        out_specs=[pl.BlockSpec(memory_space=pltpu.VMEM)] * len(outs),
        compiler_params=pltpu.CompilerParams(vmem_limit_bytes=vmem),
        cost_estimate=pl.CostEstimate(flops=flops, bytes_accessed=moved, transcendentals=0),
    )(ids, *arrays)


def shaped(*shape):
    return jax.ShapeDtypeStruct(shape, F32)


def prior_kernel(half_ref, upper_ref, solved_ref, out_ref):
    @pl.when(pl.program_id(0) == 0)
    def _():
        out_ref[...] = jnp.zeros_like(out_ref)

    width = solved_ref.shape[2]
    right = jnp.concatenate([solved_ref[0], solved_ref[1]], axis=1)
    high, low = split(right)

    def apply(left):
        left_high, left_low = split(left)
        return dot(left_high, high) + (dot(left_high, low) + dot(left_low, high))

    real = apply(upper_ref[0, 0])
    imag = apply(upper_ref[1, 0])
    out_ref[0] += real[:, :width] + imag[:, width:]
    out_ref[1] += real[:, width:] - imag[:, :width]


def prior(upper_cols, solved, panel, half, chunks=4):
    cols, depth = upper_cols.shape[2:]
    width = solved.shape[2] // 2
    step = depth // chunks
    return pl.pallas_call(
        prior_kernel,
        out_shape=shaped(2, cols, width),
        grid_spec=pltpu.PrefetchScalarGridSpec(
            num_scalar_prefetch=1,
            grid=(chunks,),
            in_specs=[
                pl.BlockSpec((2, 1, cols, step), lambda k, h: (0, panel, 0, k)),
                pl.BlockSpec((2, step, width), lambda k, h: (0, k, h[0])),
            ],
            out_specs=pl.BlockSpec((2, cols, width), lambda k, h: (0, 0, 0)),
        ),
        compiler_params=pltpu.CompilerParams(vmem_limit_bytes=24 * MIB, dimension_semantics=("arbitrary",)),
        cost_estimate=pl.CostEstimate(
            flops=24 * cols * depth * width, bytes_accessed=8 * (cols + width) * depth, transcendentals=0
        ),
    )(half, upper_cols, solved)


def near_kernel(ids, mine_ref, got_ref, keep_ref, send_ref):
    total = mine_ref[...] + got_ref[...]
    width = keep_ref.shape[2]
    first = ids[1] == 0
    low, high = total[:, :, :width], total[:, :, width:]
    keep_ref[...] = jnp.where(first, low, high)
    send_ref[...] = jnp.where(first, high, low)


def side_kernel(ids, mine_ref, got_ref, right_ref, keep_ref, send_ref):
    width = mine_ref.shape[2]
    start = pl.multiple_of((ids[0] * 2 + ids[1]) * width, width)
    right = right_ref[:, 0, :, pl.ds(start, width)]
    value = jnp.where(ids[3] == 0, right, 0.0) - (mine_ref[...] + got_ref[...])
    real, imag = value[0], value[1]
    low = lane_is_low(real.shape)
    first = jnp.where(low, real, swap_halves(imag))
    second = jnp.where(low, swap_halves(real), imag)
    keep_ref[...] = jnp.where(ids[2] == 0, first, second)
    send_ref[...] = jnp.where(ids[2] == 0, second, first)


def inverse_kernel(ids, a0, a1, a2, a3, mine_ref, got_ref, out_ref):
    rows, cols = a0.shape[1] // 2, a0.shape[2]
    right = [packed_right(mine_ref[pl.ds(j * cols, cols)] + got_ref[pl.ds(j * cols, cols)]) for j in range(2)]
    shape = (2 * rows, cols)
    place = lax.broadcasted_iota(jnp.int32, shape, 0)
    upper = place < rows
    place = place - jnp.where(upper, 0, rows)
    col_place = lax.broadcasted_iota(jnp.int32, shape, 1)
    for i, pair in enumerate(((a0, a1), (a2, a3))):
        row = ids[4] ^ (i * CORE)
        row_id = place + jnp.where(upper, row, row ^ NEAR) * rows
        total = None
        for j, block in enumerate(pair):
            col_id = col_place + (ids[5] ^ (j * SIDE)) * cols
            inside = col_id <= row_id
            term = complex_product(
                jnp.where(inside, block[0], 0.0), jnp.where(inside, block[1], 0.0), right[j], False
            )
            total = term if total is None else total + term
        out_ref[pl.ds(i * 2 * rows, 2 * rows)] = total


def couple_kernel(ids, a0, a1, a2, a3, mine_ref, got_ref, near_ref, far_ref, out_ref, answer_ref):
    cols, depth = a0.shape[1:]
    answer = mine_ref[...] + got_ref[...]
    answer_ref[...] = answer
    right = [packed_right(answer[i * depth : (i + 1) * depth]) for i in range(2)]
    for j, (first, second, base) in enumerate(((a0, a2, near_ref), (a1, a3, far_ref))):
        coupled = complex_product(first[0], first[1], right[0], True)
        coupled += complex_product(second[0], second[1], right[1], True)
        out_ref[pl.ds(j * cols, cols)] = base[...] - coupled


def unpack_kernel(ids, *refs):
    out_ref = refs[-1]
    low = None
    for panel in range(2):
        mine, other = refs[2 * panel], refs[2 * panel + 1]
        for group in range(4):
            width = mine.shape[2]
            core, near = ids[0] ^ (group // 2), ids[1] ^ (group % 2)
            start = pl.multiple_of((core * 2 + near) * width, width)
            own, far = mine[group], other[group]
            low = lane_is_low(own.shape)
            first = jnp.where(ids[2] == 0, own, far)
            second = jnp.where(ids[2] == 0, far, own)
            out_ref[0, panel, :, pl.ds(start, width)] = jnp.where(low, first, swap_halves(second))
            out_ref[1, panel, :, pl.ds(start, width)] = jnp.where(low, swap_halves(first), second)


def solution(mesh):
    def swap(value, axis, bit, name):
        with jax.named_scope(name):
            return lax.ppermute(value, axis, [(i, i ^ bit) for i in range(mesh.shape[axis])])

    def all_but_last(value, axis, bit, name):
        while 2 * bit < mesh.shape[axis]:
            value = value + swap(value, axis, bit, name)
            bit *= 2
        return value, swap(value, axis, bit, name)

    def per_device(solved, upper_cols, coupling, inverse_diag, right_side):
        row, col = lax.axis_index("row"), lax.axis_index("col")
        core, near, side, far = row & 1, (row >> 1) & 1, col & 1, row >> 2
        ids = jnp.stack([core, near, side, far, row, col]).astype(jnp.int32)
        rows, cols = inverse_diag.shape[2:]
        n_rhs = right_side.shape[3]
        wide, pack = n_rhs // 4, n_rhs // 4

        def gather_matrix(block, axis, name):
            near_block = swap(block, "row", NEAR, f"{name}_near")
            mine = jnp.concatenate([block, near_block], axis=axis)
            beside = swap(mine, "col", SIDE, f"{name}_side")
            return (
                mine,
                beside,
                swap(mine, "row", CORE, f"{name}_core0"),
                swap(beside, "row", CORE, f"{name}_core1"),
            )

        def prior_terms(panel):
            name = f"prior{panel}"
            with jax.named_scope(f"{name}_send"):
                send = prior(upper_cols, solved, panel, (1 - core)[None].astype(jnp.int32))
            got = swap(send, "row", CORE, f"{name}_core")
            with jax.named_scope(f"{name}_keep"):
                mine = prior(upper_cols, solved, panel, core[None].astype(jnp.int32))
            with jax.named_scope(f"{name}_split"):
                keep, send = call(near_kernel, ids, (mine, got), [shaped(2, cols, wide)] * 2)
            got = swap(send, "row", NEAR, f"{name}_near")
            right = right_side[:, panel : panel + 1]
            with jax.named_scope(f"{name}_pack"):
                keep, send = call(side_kernel, ids, (keep, got, right), [shaped(cols, pack)] * 2)
            return keep, swap(send, "col", SIDE, f"{name}_side")

        def apply_inverse(blocks, mine, got, name):
            with jax.named_scope(name):
                (part,) = call(
                    inverse_kernel, ids, (*blocks, mine, got), [shaped(4 * rows, pack)], 24 * MIB, 48 * rows * cols * pack
                )
            return all_but_last(part, "col", 2 * SIDE, f"{name}_sum")

        def spread(answer, name):
            parts = [answer[i * rows : (i + 1) * rows] for i in range(4)]
            got = swap(jnp.concatenate([parts[1], parts[3]], axis=0), "row", NEAR, f"{name}_near")
            other = swap(jnp.stack([parts[2], got[rows:]]), "row", CORE, f"{name}_core")
            mine = jnp.concatenate([jnp.stack([parts[0], got[:rows]]), other], axis=0)
            return mine, swap(mine, "col", SIDE, f"{name}_side")

        inverse0 = gather_matrix(inverse_diag[:, 0], 1, "inverse0")
        couple = gather_matrix(coupling, 2, "couple")
        inverse1 = gather_matrix(inverse_diag[:, 1], 1, "inverse1")

        keep, beside = prior_terms(0)
        mine, got = all_but_last(jnp.concatenate([keep, beside], axis=0), "row", 2 * NEAR, "first_far")
        part, got = apply_inverse(inverse0, mine, got, "first")
        keep1, beside1 = prior_terms(1)
        with jax.named_scope("couple"):
            mine, answer0 = call(
                couple_kernel,
                ids,
                (*couple, part, got, keep1, beside1),
                [shaped(2 * cols, pack), shaped(4 * rows, pack)],
                24 * MIB,
                48 * rows * cols * pack,
            )
        spread0 = spread(answer0, "spread0")
        mine, got = all_but_last(mine, "row", 2 * NEAR, "second_far")
        part, got = apply_inverse(inverse1, mine, got, "second")
        spread1 = spread(part + got, "spread1")
        with jax.named_scope("unpack"):
            (out,) = call(unpack_kernel, ids, (*spread0, *spread1), [shaped(2, 2, rows, n_rhs)])
        return out

    in_specs = (
        P(None, "row", None),
        P(None, None, "col", "row"),
        P(None, "col", "row"),
        P(None, None, "row", "col"),
        P(None, None, "col", None),
    )
    return jax.shard_map(
        per_device, mesh=mesh, in_specs=in_specs, out_specs=P(None, None, "row", None), check_vma=False
    )
```

```python
import functools

import jax
import jax.numpy as jnp
from jax import lax
from jax.experimental import pallas as pl
from jax.experimental.pallas import tpu as pltpu
from jax.sharding import PartitionSpec as P


CORE = 1
NEAR = 2
SIDE = 1
F32 = jnp.float32
BF16 = jnp.bfloat16
MIB = 1 << 20


def split(value):
    high = value.astype(BF16)
    return high, (value - high.astype(F32)).astype(BF16)


def dot(left, right):
    return jnp.dot(left, right, preferred_element_type=F32)


def product(left, right):
    (high, low), (both, right_high) = left, right
    width = right_high.shape[1]
    full = dot(high, both)
    return full[:, :width] + (full[:, width:] + dot(low, right_high))


def packed_right(value):
    high, low = split(value)
    return jnp.concatenate([high, low], axis=1), high


def lane_is_low(shape):
    return lax.broadcasted_iota(jnp.int32, shape, 1) < shape[1] // 2


def swap_halves(value):
    return pltpu.roll(value, value.shape[1] // 2, 1)


def complex_product(real, imag, right, conj):
    plain = product(split(real), right)
    cross = swap_halves(product(split(imag), right))
    low = lane_is_low(plain.shape)
    return plain + jnp.where(low if conj else jnp.logical_not(low), cross, -cross)


def call(kernel, ids, arrays, outs, vmem=12 * MIB, flops=0):
    moved = sum(a.size * 4 for a in arrays) + sum(4 * o.size for o in outs)
    return pl.pallas_call(
        kernel,
        out_shape=outs,
        in_specs=[pl.BlockSpec(memory_space=pltpu.SMEM)] + [pl.BlockSpec(memory_space=pltpu.VMEM)] * len(arrays),
        out_specs=[pl.BlockSpec(memory_space=pltpu.VMEM)] * len(outs),
        compiler_params=pltpu.CompilerParams(vmem_limit_bytes=vmem),
        cost_estimate=pl.CostEstimate(flops=flops, bytes_accessed=moved, transcendentals=0),
    )(ids, *arrays)


def shaped(*shape):
    return jax.ShapeDtypeStruct(shape, F32)


def prior_kernel(panel, chunks, ids, upper, solved, keep_ref, send_ref, factor, value, total, factor_sems, value_sems):
    step, width = value.shape[1] // chunks, keep_ref.shape[2]
    copies = []
    for i in range(chunks):
        place = pl.ds(i * step, step)
        copies.append(
            (
                pltpu.make_async_copy(upper.at[:, panel, :, place], factor.at[:, :, place], factor_sems.at[i]),
                pltpu.make_async_copy(solved.at[:, place], value.at[:, place], value_sems.at[i]),
            )
        )
    for pair in copies:
        for copy in pair:
            copy.start()

    def multiply(left, right):
        (left_high, left_low), (right_high, right_low) = split(left), split(right)
        return dot(left_high, right_high) + (dot(left_high, right_low) + dot(left_low, right_high))

    for i, pair in enumerate(copies):
        for copy in pair:
            copy.wait()
        place = pl.ds(i * step, step)
        left_real, left_imag = factor[0, :, place], factor[1, :, place]
        right_real, right_imag = value[0, place], value[1, place]
        first = multiply(left_real, right_real)
        second = multiply(left_imag, right_imag)
        mixed = multiply(left_real - left_imag, right_real + right_imag)
        real, imag = first + second, mixed - first + second
        total[0] = real if i == 0 else total[0] + real
        total[1] = imag if i == 0 else total[1] + imag
    low, high = total[:, :, :width], total[:, :, width:]
    keep_ref[...] = jnp.where(ids[0] == 0, low, high)
    send_ref[...] = jnp.where(ids[0] == 0, high, low)


def prior(ids, upper_cols, solved, panel, chunks=4):
    cols, depth = upper_cols.shape[2:]
    width = solved.shape[2]
    return pl.pallas_call(
        functools.partial(prior_kernel, panel, chunks),
        out_shape=[shaped(2, cols, width // 2)] * 2,
        in_specs=[pl.BlockSpec(memory_space=pltpu.SMEM)] + [pl.BlockSpec(memory_space=pl.ANY)] * 2,
        out_specs=[pl.BlockSpec(memory_space=pltpu.VMEM)] * 2,
        scratch_shapes=[
            pltpu.VMEM((2, cols, depth), F32),
            pltpu.VMEM((2, depth, width), F32),
            pltpu.VMEM((2, cols, width), F32),
            pltpu.SemaphoreType.DMA((chunks,)),
            pltpu.SemaphoreType.DMA((chunks,)),
        ],
        compiler_params=pltpu.CompilerParams(vmem_limit_bytes=52 * MIB),
        cost_estimate=pl.CostEstimate(
            flops=18 * cols * depth * width, bytes_accessed=8 * (cols + width) * depth, transcendentals=0
        ),
    )(ids, upper_cols, solved)


def pack(real, imag, near):
    low = lane_is_low(real.shape)
    first = jnp.where(low, real, swap_halves(imag))
    second = jnp.where(low, swap_halves(real), imag)
    return jnp.where(near == 0, first, second), jnp.where(near == 0, second, first)


def terms(ids, mine_ref, got_ref, right_ref):
    width = mine_ref.shape[2]
    right = right_ref[:, 0, :, pl.ds(pl.multiple_of(ids[0] * width, width), width)]
    return jnp.where((ids[1] == 0) & (ids[3] == 0), right, 0.0) - (mine_ref[...] + got_ref[...])


def split_kernel(ids, mine_ref, got_ref, right_ref, beside_ref, keep_ref, send_ref):
    value = terms(ids, mine_ref, got_ref, right_ref)
    width = beside_ref.shape[2]
    low, high = value[:, :, :width], value[:, :, width:]
    beside_ref[...] = jnp.where(ids[2] == 0, high, low)
    keep = jnp.where(ids[2] == 0, low, high)
    keep_ref[...], send_ref[...] = pack(keep[0], keep[1], ids[1])


def pack_kernel(ids, value_ref, keep_ref, send_ref):
    keep_ref[...], send_ref[...] = pack(value_ref[0], value_ref[1], ids[1])


def split_both_kernel(ids, mine_ref, got_ref, right_ref, keep_ref, send_ref):
    value = terms(ids, mine_ref, got_ref, right_ref)
    width = keep_ref.shape[2]
    for i in range(2):
        part = value[:, :, i * width : (i + 1) * width]
        keep_ref[i], send_ref[i] = pack(part[0], part[1], ids[1])


def pick_kernel(ids, mine_ref, got_ref, keep_ref, send_ref):
    first, second = mine_ref[0] + got_ref[0], mine_ref[1] + got_ref[1]
    keep_ref[...] = jnp.where(ids[2] == 0, first, second)
    send_ref[...] = jnp.where(ids[2] == 0, second, first)


def inverse_kernel(ids, a0, a1, a2, a3, *refs):
    out_ref, pieces = refs[-1], len(refs) // 2
    rows, cols = a0.shape[1] // 2, a0.shape[2]
    value = jnp.concatenate([refs[i][...] + refs[pieces + i][...] for i in range(pieces)], axis=0)
    right = [packed_right(value[j * cols : (j + 1) * cols]) for j in range(2)]
    shape = (2 * rows, cols)
    place = lax.broadcasted_iota(jnp.int32, shape, 0)
    upper = place < rows
    place = place - jnp.where(upper, 0, rows)
    col_place = lax.broadcasted_iota(jnp.int32, shape, 1)
    for i, pair in enumerate(((a0, a1), (a2, a3))):
        row = ids[4] ^ (i * CORE)
        row_id = place + jnp.where(upper, row, row ^ NEAR) * rows
        total = None
        for j, block in enumerate(pair):
            col_id = col_place + (ids[5] ^ (j * SIDE)) * cols
            inside = col_id <= row_id
            term = complex_product(
                jnp.where(inside, block[0], 0.0), jnp.where(inside, block[1], 0.0), right[j], False
            )
            total = term if total is None else total + term
        out_ref[pl.ds(i * 2 * rows, 2 * rows)] = total


def couple_kernel(ids, a0, a1, a2, a3, mine_ref, got_ref, near_ref, far_ref, out_ref, answer_ref):
    cols, depth = near_ref.shape[0], 2 * a0.shape[2]
    answer = mine_ref[...] + got_ref[...]
    answer_ref[...] = answer
    right = [packed_right(answer[i * depth : (i + 1) * depth]) for i in range(2)]
    for j, base in enumerate((near_ref, far_ref)):
        value = base[...]
        for i, block in enumerate((a0, a2) if j == 0 else (a1, a3)):
            real, imag = (
                jnp.concatenate([block[part, pl.ds(near * cols, cols)] for near in range(2)], axis=1)
                for part in range(2)
            )
            value -= complex_product(real, imag, right[i], True)
        out_ref[pl.ds(j * cols, cols)] = value


def unpack_kernel(flips, panel, ids, *refs):
    out_ref, blocks, sem = refs[-3:]
    copies = []
    for flip, own_ref, far_ref in zip(flips, refs[0::2], refs[1::2]):
        rows, width = own_ref.shape[0] // 2, own_ref.shape[1]
        for i in range(2):
            own, far = own_ref[pl.ds(i * rows, rows)], far_ref[pl.ds(i * rows, rows)]
            low = lane_is_low(own.shape)
            start = pl.multiple_of(((ids[0] ^ i) * 2 + (ids[2] ^ flip)) * width, width)
            first = jnp.where(ids[1] == 0, own, far)
            second = jnp.where(ids[1] == 0, far, own)
            block = blocks.at[len(copies)]
            block[0] = jnp.where(low, first, swap_halves(second))
            block[1] = jnp.where(low, swap_halves(first), second)
            copies.append(
                pltpu.make_async_copy(block, out_ref.at[:, panel, :, pl.ds(start, width)], sem.at[len(copies)])
            )
            copies[-1].start()
    for copy in copies:
        copy.wait()


def unpack(ids, pairs, panel, flips, out=None):
    rows, width = pairs[0].shape[0] // 2, pairs[0].shape[1]
    given = [] if out is None else [out]
    return pl.pallas_call(
        functools.partial(unpack_kernel, flips, panel),
        out_shape=shaped(2, 2, rows, 4 * width),
        in_specs=[
            pl.BlockSpec(memory_space=pltpu.SMEM),
            *([pl.BlockSpec(memory_space=pltpu.VMEM)] * len(pairs)),
            *([pl.BlockSpec(memory_space=pl.ANY)] * len(given)),
        ],
        out_specs=pl.BlockSpec(memory_space=pl.ANY),
        scratch_shapes=[pltpu.VMEM((len(pairs), 2, rows, width), F32), pltpu.SemaphoreType.DMA((len(pairs),))],
        input_output_aliases={1 + len(pairs): 0} if given else {},
        compiler_params=pltpu.CompilerParams(vmem_limit_bytes=8 * MIB),
        cost_estimate=pl.CostEstimate(flops=0, bytes_accessed=8 * sum(p.size for p in pairs), transcendentals=0),
    )(ids, *pairs, *given)


def solution(mesh):
    def swap(value, axis, bit):
        return lax.ppermute(value, axis, [(i, i ^ bit) for i in range(mesh.shape[axis])])

    def all_but_last(value, axis, bit):
        while 2 * bit < mesh.shape[axis]:
            value = value + swap(value, axis, bit)
            bit *= 2
        return value, swap(value, axis, bit)

    def per_device(solved, upper_cols, coupling, inverse_diag, right_side):
        row, col = lax.axis_index("row"), lax.axis_index("col")
        core, near, side, far = row & 1, (row >> 1) & 1, col & 1, row >> 2
        ids = jnp.stack([core, near, side, far, row, col]).astype(jnp.int32)
        rows, cols = inverse_diag.shape[2:]
        n_rhs = right_side.shape[3]
        wide = n_rhs // 4

        def gather_matrix(block):
            near_block = swap(block, "row", NEAR)
            mine = jnp.concatenate([block, near_block], axis=1)
            beside = swap(mine, "col", SIDE)
            return (mine, beside, swap(mine, "row", CORE), swap(beside, "row", CORE))

        def chip_terms(panel):
            mine, send = prior(ids, upper_cols, solved, panel)
            return mine, swap(send, "row", CORE), right_side[:, panel : panel + 1]

        def first_terms():
            shapes = [shaped(2, cols, wide), shaped(cols, wide), shaped(cols, wide)]
            given = chip_terms(0)
            beside, keep, send = call(split_kernel, ids, given, shapes)
            beside = swap(beside, "col", SIDE)
            mine = keep + swap(send, "row", NEAR)
            keep, send = call(pack_kernel, ids, (beside,), shapes[1:])
            return mine, keep + swap(send, "row", NEAR)

        def second_terms():
            given = chip_terms(1)
            keep, send = call(split_both_kernel, ids, given, [shaped(2, cols, wide)] * 2)
            got = swap(send, "row", NEAR)
            keep, send = call(pick_kernel, ids, (keep, got), [shaped(cols, wide)] * 2)
            return keep, swap(send, "col", SIDE)

        def apply_inverse(blocks, mine, got):
            (part,) = call(
                inverse_kernel, ids, (*blocks, *mine, *got), [shaped(4 * rows, wide)], 24 * MIB, 48 * rows * cols * wide
            )
            return all_but_last(part, "col", 2 * SIDE)

        def spread(answer):
            parts = [answer[i * rows : (i + 1) * rows] for i in range(4)]
            got = swap(jnp.concatenate([parts[2], parts[3]], axis=0), "row", CORE)
            far = swap(jnp.concatenate([parts[1], got[rows:]], axis=0), "row", NEAR)
            mine = jnp.concatenate([parts[0], got[:rows]], axis=0)
            return (mine, far), [swap(v, "col", SIDE) for v in (mine, far)]

        inverse0 = gather_matrix(inverse_diag[:, 0])
        couple = gather_matrix(coupling)
        inverse1 = gather_matrix(inverse_diag[:, 1])

        pieces = [all_but_last(v, "row", 2 * NEAR) for v in first_terms()]
        part, got = apply_inverse(inverse0, *zip(*pieces))
        keep1, beside1 = second_terms()
        mine, answer0 = call(
            couple_kernel,
            ids,
            (*couple, part, got, keep1, beside1),
            [shaped(2 * cols, wide), shaped(4 * rows, wide)],
            24 * MIB,
            48 * rows * cols * wide,
        )
        mine0, other0 = spread(answer0)
        mine, got = all_but_last(mine, "row", 2 * NEAR)
        part, got = apply_inverse(inverse1, (mine,), (got,))
        out = unpack(ids, (*mine0, *other0), 0, (0, 1))
        mine1, other1 = spread(part + got)
        out = unpack(ids, mine1, 1, (0,), out)
        return unpack(ids, other1, 1, (1,), out)

    in_specs = (
        P(None, "row", None),
        P(None, None, "col", "row"),
        P(None, "col", "row"),
        P(None, None, "row", "col"),
        P(None, None, "col", None),
    )

    return jax.shard_map(
        per_device, mesh=mesh, in_specs=in_specs, out_specs=P(None, None, "row", None), check_vma=False
    )
```

```python
import functools

import jax
import jax.numpy as jnp
from jax import lax
from jax.experimental import pallas as pl
from jax.experimental.pallas import tpu as pltpu
from jax.sharding import PartitionSpec as P


CORE = 1
NEAR = 2
SIDE = 1
F32 = jnp.float32
BF16 = jnp.bfloat16
MIB = 1 << 20


def split(value):
    high = value.astype(BF16)
    return high, (value - high.astype(F32)).astype(BF16)


def dot(left, right):
    return jnp.dot(left, right, preferred_element_type=F32)


def product(left, right):
    (high, low), (both, right_high) = left, right
    width = right_high.shape[1]
    full = dot(high, both)
    return full[:, :width] + (full[:, width:] + dot(low, right_high))


def packed_right(value):
    high, low = split(value)
    return jnp.concatenate([high, low], axis=1), high


def lane_is_low(shape):
    return lax.broadcasted_iota(jnp.int32, shape, 1) < shape[1] // 2


def swap_halves(value):
    return pltpu.roll(value, value.shape[1] // 2, 1)


def complex_product(real, imag, right, conj):
    plain = product(split(real), right)
    cross = swap_halves(product(split(imag), right))
    low = lane_is_low(plain.shape)
    return plain + jnp.where(low if conj else jnp.logical_not(low), cross, -cross)


def call(kernel, ids, arrays, outs, vmem=12 * MIB, flops=0):
    moved = sum(a.size * 4 for a in arrays) + sum(4 * o.size for o in outs)
    return pl.pallas_call(
        kernel,
        out_shape=outs,
        in_specs=[pl.BlockSpec(memory_space=pltpu.SMEM)] + [pl.BlockSpec(memory_space=pltpu.VMEM)] * len(arrays),
        out_specs=[pl.BlockSpec(memory_space=pltpu.VMEM)] * len(outs),
        compiler_params=pltpu.CompilerParams(vmem_limit_bytes=vmem),
        cost_estimate=pl.CostEstimate(flops=flops, bytes_accessed=moved, transcendentals=0),
    )(ids, *arrays)


def shaped(*shape):
    return jax.ShapeDtypeStruct(shape, F32)


def multiply(left, right):
    (left_high, left_low), (right_high, right_low) = split(left), split(right)
    return dot(left_high, right_high) + (dot(left_high, right_low) + dot(left_low, right_high))


def prior_kernel(panel, chunks, ids, upper, solved, keep_ref, send_ref, total, *scratch):
    step, width = solved.shape[1] // chunks, keep_ref.shape[2]
    places = [pl.ds(i * step, step) for i in range(chunks)]
    copies = []
    if scratch:
        factor, value, factor_sems, value_sems = scratch
        for i, place in enumerate(places):
            copies += [
                pltpu.make_async_copy(upper.at[:, pl.ds(panel, 1), :, place], factor.at[:, :, :, place], factor_sems.at[i]),
                pltpu.make_async_copy(solved.at[:, place], value.at[:, place], value_sems.at[i]),
            ]
        upper, solved, panel = factor, value, 0
    for copy in copies:
        copy.start()
    for i, place in enumerate(places):
        for copy in copies[2 * i : 2 * i + 2]:
            copy.wait()
        left_real, left_imag = upper[0, panel, :, place], upper[1, panel, :, place]
        right_real, right_imag = solved[0, place], solved[1, place]
        first = multiply(left_real, right_real)
        second = multiply(left_imag, right_imag)
        mixed = multiply(left_real - left_imag, right_real + right_imag)
        real, imag = first + second, mixed - first + second
        total[0] = real if i == 0 else total[0] + real
        total[1] = imag if i == 0 else total[1] + imag
    low, high = total[:, :, :width], total[:, :, width:]
    keep_ref[...] = jnp.where(ids[0] == 0, low, high)
    send_ref[...] = jnp.where(ids[0] == 0, high, low)


def prior(ids, upper_cols, solved, panel, own_copies, chunks=4):
    cols, depth = upper_cols.shape[2:]
    width = solved.shape[2]
    scratch = [
        pltpu.VMEM((2, 1, cols, depth), F32),
        pltpu.VMEM((2, depth, width), F32),
        pltpu.SemaphoreType.DMA((chunks,)),
        pltpu.SemaphoreType.DMA((chunks,)),
    ]
    space = pl.ANY if own_copies else pltpu.VMEM
    return pl.pallas_call(
        functools.partial(prior_kernel, panel, chunks),
        out_shape=[shaped(2, cols, width // 2)] * 2,
        in_specs=[pl.BlockSpec(memory_space=pltpu.SMEM)] + [pl.BlockSpec(memory_space=space)] * 2,
        out_specs=[pl.BlockSpec(memory_space=pltpu.VMEM)] * 2,
        scratch_shapes=[pltpu.VMEM((2, cols, width), F32)] + (scratch if own_copies else []),
        compiler_params=pltpu.CompilerParams(vmem_limit_bytes=(52 if own_copies else 24) * MIB),
        cost_estimate=pl.CostEstimate(
            flops=18 * cols * depth * width, bytes_accessed=8 * (cols + width) * depth, transcendentals=0
        ),
    )(ids, upper_cols, solved)


def pack(real, imag, near):
    low = lane_is_low(real.shape)
    first = jnp.where(low, real, swap_halves(imag))
    second = jnp.where(low, swap_halves(real), imag)
    return jnp.where(near == 0, first, second), jnp.where(near == 0, second, first)


def terms(ids, mine_ref, got_ref, right_ref):
    width = mine_ref.shape[2]
    right = right_ref[:, 0, :, pl.ds(pl.multiple_of(ids[0] * width, width), width)]
    return jnp.where((ids[1] == 0) & (ids[3] == 0), right, 0.0) - (mine_ref[...] + got_ref[...])


def split_kernel(ids, mine_ref, got_ref, right_ref, beside_ref, keep_ref, send_ref):
    value = terms(ids, mine_ref, got_ref, right_ref)
    width = beside_ref.shape[2]
    low, high = value[:, :, :width], value[:, :, width:]
    beside_ref[...] = jnp.where(ids[2] == 0, high, low)
    keep = jnp.where(ids[2] == 0, low, high)
    keep_ref[...], send_ref[...] = pack(keep[0], keep[1], ids[1])


def pack_kernel(ids, value_ref, keep_ref, send_ref):
    keep_ref[...], send_ref[...] = pack(value_ref[0], value_ref[1], ids[1])


def split_both_kernel(ids, mine_ref, got_ref, right_ref, keep_ref, send_ref):
    value = terms(ids, mine_ref, got_ref, right_ref)
    width = keep_ref.shape[2]
    for i in range(2):
        part = value[:, :, i * width : (i + 1) * width]
        keep_ref[i], send_ref[i] = pack(part[0], part[1], ids[1])


def pick_kernel(ids, mine_ref, got_ref, keep_ref, send_ref):
    first, second = mine_ref[0] + got_ref[0], mine_ref[1] + got_ref[1]
    keep_ref[...] = jnp.where(ids[2] == 0, first, second)
    send_ref[...] = jnp.where(ids[2] == 0, second, first)


def inverse_kernel(ids, a0, a1, a2, a3, *refs):
    out_ref, pieces = refs[-1], len(refs) // 2
    rows, cols = a0.shape[1] // 2, a0.shape[2]
    value = jnp.concatenate([refs[i][...] + refs[pieces + i][...] for i in range(pieces)], axis=0)
    right = [packed_right(value[j * cols : (j + 1) * cols]) for j in range(2)]
    shape = (2 * rows, cols)
    place = lax.broadcasted_iota(jnp.int32, shape, 0)
    upper = place < rows
    place = place - jnp.where(upper, 0, rows)
    col_place = lax.broadcasted_iota(jnp.int32, shape, 1)
    for i, pair in enumerate(((a0, a1), (a2, a3))):
        row = ids[4] ^ (i * CORE)
        row_id = place + jnp.where(upper, row, row ^ NEAR) * rows
        total = None
        for j, block in enumerate(pair):
            col_id = col_place + (ids[5] ^ (j * SIDE)) * cols
            inside = col_id <= row_id
            term = complex_product(
                jnp.where(inside, block[0], 0.0), jnp.where(inside, block[1], 0.0), right[j], False
            )
            total = term if total is None else total + term
        out_ref[pl.ds(i * 2 * rows, 2 * rows)] = total


def couple_kernel(ids, a0, a1, a2, a3, mine_ref, got_ref, near_ref, far_ref, out_ref, answer_ref):
    cols, depth = near_ref.shape[0], 2 * a0.shape[2]
    answer = mine_ref[...] + got_ref[...]
    answer_ref[...] = answer
    right = [packed_right(answer[i * depth : (i + 1) * depth]) for i in range(2)]
    for j, base in enumerate((near_ref, far_ref)):
        value = base[...]
        for i, block in enumerate((a0, a2) if j == 0 else (a1, a3)):
            real, imag = (
                jnp.concatenate([block[part, pl.ds(near * cols, cols)] for near in range(2)], axis=1)
                for part in range(2)
            )
            value -= complex_product(real, imag, right[i], True)
        out_ref[pl.ds(j * cols, cols)] = value


def unpack_kernel(flips, panel, ids, *refs):
    out_ref, blocks, sem = refs[-3:]
    copies = []
    for flip, own_ref, far_ref in zip(flips, refs[0::2], refs[1::2]):
        rows, width = own_ref.shape[0] // 2, own_ref.shape[1]
        for i in range(2):
            own, far = own_ref[pl.ds(i * rows, rows)], far_ref[pl.ds(i * rows, rows)]
            low = lane_is_low(own.shape)
            start = pl.multiple_of(((ids[0] ^ i) * 2 + (ids[2] ^ flip)) * width, width)
            first = jnp.where(ids[1] == 0, own, far)
            second = jnp.where(ids[1] == 0, far, own)
            block = blocks.at[len(copies)]
            block[0] = jnp.where(low, first, swap_halves(second))
            block[1] = jnp.where(low, swap_halves(first), second)
            copies.append(
                pltpu.make_async_copy(block, out_ref.at[:, panel, :, pl.ds(start, width)], sem.at[len(copies)])
            )
            copies[-1].start()
    for copy in copies:
        copy.wait()


def unpack(ids, pairs, panel, flips, out=None):
    rows, width = pairs[0].shape[0] // 2, pairs[0].shape[1]
    given = [] if out is None else [out]
    return pl.pallas_call(
        functools.partial(unpack_kernel, flips, panel),
        out_shape=shaped(2, 2, rows, 4 * width),
        in_specs=[
            pl.BlockSpec(memory_space=pltpu.SMEM),
            *([pl.BlockSpec(memory_space=pltpu.VMEM)] * len(pairs)),
            *([pl.BlockSpec(memory_space=pl.ANY)] * len(given)),
        ],
        out_specs=pl.BlockSpec(memory_space=pl.ANY),
        scratch_shapes=[pltpu.VMEM((len(pairs), 2, rows, width), F32), pltpu.SemaphoreType.DMA((len(pairs),))],
        input_output_aliases={1 + len(pairs): 0} if given else {},
        compiler_params=pltpu.CompilerParams(vmem_limit_bytes=8 * MIB),
        cost_estimate=pl.CostEstimate(flops=0, bytes_accessed=8 * sum(p.size for p in pairs), transcendentals=0),
    )(ids, *pairs, *given)


def solution(mesh):
    def swap(value, axis, bit):
        return lax.ppermute(value, axis, [(i, i ^ bit) for i in range(mesh.shape[axis])])

    def all_but_last(value, axis, bit):
        while 2 * bit < mesh.shape[axis]:
            value = value + swap(value, axis, bit)
            bit *= 2
        return value, swap(value, axis, bit)

    def per_device(solved, upper_cols, coupling, inverse_diag, right_side):
        row, col = lax.axis_index("row"), lax.axis_index("col")
        core, near, side, far = row & 1, (row >> 1) & 1, col & 1, row >> 2
        ids = jnp.stack([core, near, side, far, row, col]).astype(jnp.int32)
        rows, cols = inverse_diag.shape[2:]
        n_rhs = right_side.shape[3]
        wide = n_rhs // 4

        def gather_matrix(block):
            got = swap(block, "row", NEAR)
            mine = jnp.concatenate([block, got], axis=1)
            beside = swap(mine, "col", SIDE)
            return (mine, beside, swap(mine, "row", CORE), swap(beside, "row", CORE))

        def chip_terms(panel):
            mine, send = prior(ids, upper_cols, solved, panel, panel == 0)
            return mine, swap(send, "row", CORE), right_side[:, panel : panel + 1]

        def first_terms():
            shapes = [shaped(2, cols, wide), shaped(cols, wide), shaped(cols, wide)]
            given = chip_terms(0)
            beside, keep, send = call(split_kernel, ids, given, shapes)
            beside = swap(beside, "col", SIDE)
            mine = keep + swap(send, "row", NEAR)
            keep, send = call(pack_kernel, ids, (beside,), shapes[1:])
            return mine, keep + swap(send, "row", NEAR)

        def second_terms():
            given = chip_terms(1)
            keep, send = call(split_both_kernel, ids, given, [shaped(2, cols, wide)] * 2)
            got = swap(send, "row", NEAR)
            keep, send = call(pick_kernel, ids, (keep, got), [shaped(cols, wide)] * 2)
            return keep, swap(send, "col", SIDE)

        def apply_inverse(blocks, mine, got):
            return call(
                inverse_kernel, ids, (*blocks, *mine, *got), [shaped(4 * rows, wide)], 24 * MIB, 48 * rows * cols * wide
            )[0]

        def spread(answer, partial=False):
            parts = [answer[i * rows : (i + 1) * rows] for i in range(4)]
            got = swap(jnp.concatenate([parts[2], parts[3]], axis=0), "row", CORE)
            far = swap(jnp.concatenate([parts[1], got[rows:]], axis=0), "row", NEAR)
            mine = [jnp.concatenate([parts[0], got[:rows]], axis=0), far]
            if partial:
                mine = [sum(all_but_last(v, "col", 2 * SIDE)) for v in mine]
            return mine, [swap(v, "col", SIDE) for v in mine]

        inverse0 = gather_matrix(inverse_diag[:, 0])
        couple = gather_matrix(coupling)
        inverse1 = gather_matrix(inverse_diag[:, 1])

        pieces = [all_but_last(v, "row", 2 * NEAR) for v in first_terms()]
        part, got = all_but_last(apply_inverse(inverse0, *zip(*pieces)), "col", 2 * SIDE)
        keep1, beside1 = second_terms()
        mine, answer0 = call(
            couple_kernel,
            ids,
            (*couple, part, got, keep1, beside1),
            [shaped(2 * cols, wide), shaped(4 * rows, wide)],
            24 * MIB,
            48 * rows * cols * wide,
        )
        mine0, other0 = spread(answer0)
        mine, got = all_but_last(mine, "row", 2 * NEAR)
        part = apply_inverse(inverse1, (mine,), (got,))
        out = unpack(ids, (*mine0, *other0), 0, (0, 1))
        mine1, other1 = spread(part, True)
        out = unpack(ids, mine1, 1, (0,), out)
        return unpack(ids, other1, 1, (1,), out)

    in_specs = (
        P(None, "row", None),
        P(None, None, "col", "row"),
        P(None, "col", "row"),
        P(None, None, "row", "col"),
        P(None, None, "col", None),
    )

    return jax.shard_map(
        per_device, mesh=mesh, in_specs=in_specs, out_specs=P(None, None, "row", None), check_vma=False
    )
```

```python
import functools

import jax
import jax.numpy as jnp
from jax import lax
from jax.experimental import pallas as pl
from jax.experimental.pallas import tpu as pltpu
from jax.sharding import PartitionSpec as P


CORE = 1
NEAR = 2
SIDE = 1
F32 = jnp.float32
BF16 = jnp.bfloat16
MIB = 1 << 20


def split(value):
    high = value.astype(BF16)
    return high, (value - high.astype(F32)).astype(BF16)


def dot(left, right):
    return jnp.dot(left, right, preferred_element_type=F32)


def product(left, right):
    (high, low), (both, right_high) = left, right
    width = right_high.shape[1]
    full = dot(high, both)
    return full[:, :width] + (full[:, width:] + dot(low, right_high))


def packed_right(value):
    high, low = split(value)
    return jnp.concatenate([high, low], axis=1), high


def lane_is_low(shape):
    return lax.broadcasted_iota(jnp.int32, shape, 1) < shape[1] // 2


def swap_halves(value):
    return pltpu.roll(value, value.shape[1] // 2, 1)


def complex_product(real, imag, right, conj):
    plain = product(split(real), right)
    cross = swap_halves(product(split(imag), right))
    low = lane_is_low(plain.shape)
    return plain + jnp.where(low if conj else jnp.logical_not(low), cross, -cross)


def place():
    row, col = lax.axis_index("row"), lax.axis_index("col")
    return row & 1, (row >> 1) & 1, col & 1, row >> 2, row, col


def call(kernel, arrays, outs, vmem=12 * MIB, flops=0):
    moved = sum(a.size * 4 for a in arrays) + sum(4 * o.size for o in outs)
    return pl.pallas_call(
        kernel,
        out_shape=outs,
        in_specs=[pl.BlockSpec(memory_space=pltpu.VMEM)] * len(arrays),
        out_specs=[pl.BlockSpec(memory_space=pltpu.VMEM)] * len(outs),
        compiler_params=pltpu.CompilerParams(vmem_limit_bytes=vmem),
        cost_estimate=pl.CostEstimate(flops=flops, bytes_accessed=moved, transcendentals=0),
    )(*arrays)


def shaped(*shape):
    return jax.ShapeDtypeStruct(shape, F32)


def multiply(left, right):
    (left_high, left_low), (right_high, right_low) = split(left), split(right)
    return dot(left_high, right_high) + (dot(left_high, right_low) + dot(left_low, right_high))


def prior_kernel(panel, chunks, upper, solved, keep_ref, send_ref, total, *scratch):
    step, width = solved.shape[1] // chunks, keep_ref.shape[2]
    spans = [pl.ds(i * step, step) for i in range(chunks)]
    copies = []
    if scratch:
        factor, value, factor_sems, value_sems = scratch
        for i, span in enumerate(spans):
            copies += [
                pltpu.make_async_copy(upper.at[:, pl.ds(panel, 1), :, span], factor.at[:, :, :, span], factor_sems.at[i]),
                pltpu.make_async_copy(solved.at[:, span], value.at[:, span], value_sems.at[i]),
            ]
        upper, solved, panel = factor, value, 0
    for copy in copies:
        copy.start()
    for i, span in enumerate(spans):
        for copy in copies[2 * i : 2 * i + 2]:
            copy.wait()
        left_real, left_imag = upper[0, panel, :, span], upper[1, panel, :, span]
        right_real, right_imag = solved[0, span], solved[1, span]
        first = multiply(left_real, right_real)
        second = multiply(left_imag, right_imag)
        mixed = multiply(left_real - left_imag, right_real + right_imag)
        real, imag = first + second, mixed - first + second
        total[0] = real if i == 0 else total[0] + real
        total[1] = imag if i == 0 else total[1] + imag
    low, high = total[:, :, :width], total[:, :, width:]
    core = place()[0]
    keep_ref[...] = jnp.where(core == 0, low, high)
    send_ref[...] = jnp.where(core == 0, high, low)


def prior(upper_cols, solved, panel, own_copies, chunks=4):
    cols, depth = upper_cols.shape[2:]
    width = solved.shape[2]
    scratch = [
        pltpu.VMEM((2, 1, cols, depth), F32),
        pltpu.VMEM((2, depth, width), F32),
        pltpu.SemaphoreType.DMA((chunks,)),
        pltpu.SemaphoreType.DMA((chunks,)),
    ]
    space = pl.ANY if own_copies else pltpu.VMEM
    return pl.pallas_call(
        functools.partial(prior_kernel, panel, chunks),
        out_shape=[shaped(2, cols, width // 2)] * 2,
        in_specs=[pl.BlockSpec(memory_space=space)] * 2,
        out_specs=[pl.BlockSpec(memory_space=pltpu.VMEM)] * 2,
        scratch_shapes=[pltpu.VMEM((2, cols, width), F32)] + (scratch if own_copies else []),
        compiler_params=pltpu.CompilerParams(vmem_limit_bytes=(52 if own_copies else 24) * MIB),
        cost_estimate=pl.CostEstimate(
            flops=18 * cols * depth * width, bytes_accessed=8 * (cols + width) * depth, transcendentals=0
        ),
    )(upper_cols, solved)


def pack(real, imag, near):
    low = lane_is_low(real.shape)
    first = jnp.where(low, real, swap_halves(imag))
    second = jnp.where(low, swap_halves(real), imag)
    return jnp.where(near == 0, first, second), jnp.where(near == 0, second, first)


def terms(ids, mine_ref, got_ref, right_ref):
    width = mine_ref.shape[2]
    right = right_ref[:, 0, :, pl.ds(pl.multiple_of(ids[0] * width, width), width)]
    return jnp.where((ids[1] == 0) & (ids[3] == 0), right, 0.0) - (mine_ref[...] + got_ref[...])


def split_kernel(mine_ref, got_ref, right_ref, beside_ref, keep_ref, send_ref):
    ids = place()
    value = terms(ids, mine_ref, got_ref, right_ref)
    width = beside_ref.shape[2]
    low, high = value[:, :, :width], value[:, :, width:]
    beside_ref[...] = jnp.where(ids[2] == 0, high, low)
    keep = jnp.where(ids[2] == 0, low, high)
    keep_ref[...], send_ref[...] = pack(keep[0], keep[1], ids[1])


def pack_kernel(value_ref, keep_ref, send_ref):
    ids = place()
    keep_ref[...], send_ref[...] = pack(value_ref[0], value_ref[1], ids[1])


def split_both_kernel(mine_ref, got_ref, right_ref, keep_ref, send_ref):
    ids = place()
    value = terms(ids, mine_ref, got_ref, right_ref)
    width = keep_ref.shape[2]
    for i in range(2):
        part = value[:, :, i * width : (i + 1) * width]
        keep_ref[i], send_ref[i] = pack(part[0], part[1], ids[1])


def pick_kernel(mine_ref, got_ref, keep_ref, send_ref):
    ids = place()
    first, second = mine_ref[0] + got_ref[0], mine_ref[1] + got_ref[1]
    keep_ref[...] = jnp.where(ids[2] == 0, first, second)
    send_ref[...] = jnp.where(ids[2] == 0, second, first)


def inverse_kernel(flips, *refs):
    ids = place()
    blocks, pieces, out_ref = refs[: 2 * len(flips)], refs[2 * len(flips) : -1], refs[-1]
    half = len(pieces) // 2
    rows, cols = blocks[0].shape[1] // 2, blocks[0].shape[2]
    value = jnp.concatenate([pieces[i][...] + pieces[half + i][...] for i in range(half)], axis=0)
    right = [packed_right(value[j * cols : (j + 1) * cols]) for j in range(2)]
    shape = (2 * rows, cols)
    row_place = lax.broadcasted_iota(jnp.int32, shape, 0)
    upper = row_place < rows
    row_place = row_place - jnp.where(upper, 0, rows)
    col_place = lax.broadcasted_iota(jnp.int32, shape, 1)
    for i, flip in enumerate(flips):
        row = ids[4] ^ (flip * CORE)
        row_id = row_place + jnp.where(upper, row, row ^ NEAR) * rows
        total = None
        for j, block in enumerate(blocks[2 * i : 2 * i + 2]):
            col_id = col_place + (ids[5] ^ (j * SIDE)) * cols
            inside = col_id <= row_id
            term = complex_product(
                jnp.where(inside, block[0], 0.0), jnp.where(inside, block[1], 0.0), right[j], False
            )
            total = term if total is None else total + term
        out_ref[pl.ds(i * 2 * rows, 2 * rows)] = total


def couple_kernel(a0, a1, a2, a3, mine_ref, got_ref, near_ref, far_ref, out_ref, answer_ref):
    cols, depth = near_ref.shape[0], 2 * a0.shape[2]
    answer = mine_ref[...] + got_ref[...]
    answer_ref[...] = answer
    right = [packed_right(answer[i * depth : (i + 1) * depth]) for i in range(2)]
    for j, base in enumerate((near_ref, far_ref)):
        value = base[...]
        for i, block in enumerate((a0, a2) if j == 0 else (a1, a3)):
            real, imag = (
                jnp.concatenate([block[part, pl.ds(near * cols, cols)] for near in range(2)], axis=1)
                for part in range(2)
            )
            value -= complex_product(real, imag, right[i], True)
        out_ref[pl.ds(j * cols, cols)] = value


def unpack_kernel(flips, panel, *refs):
    ids = place()
    out_ref, blocks, sem = refs[-3:]
    copies = []
    for flip, own_ref, far_ref in zip(flips, refs[0::2], refs[1::2]):
        rows, width = own_ref.shape[0] // 2, own_ref.shape[1]
        for i in range(2):
            own, far = own_ref[pl.ds(i * rows, rows)], far_ref[pl.ds(i * rows, rows)]
            low = lane_is_low(own.shape)
            start = pl.multiple_of(((ids[0] ^ i) * 2 + (ids[2] ^ flip)) * width, width)
            first = jnp.where(ids[1] == 0, own, far)
            second = jnp.where(ids[1] == 0, far, own)
            block = blocks.at[len(copies)]
            block[0] = jnp.where(low, first, swap_halves(second))
            block[1] = jnp.where(low, swap_halves(first), second)
            copies.append(
                pltpu.make_async_copy(block, out_ref.at[:, panel, :, pl.ds(start, width)], sem.at[len(copies)])
            )
            copies[-1].start()
    for copy in copies:
        copy.wait()


def unpack(pairs, panel, flips, out=None):
    rows, width = pairs[0].shape[0] // 2, pairs[0].shape[1]
    given = [] if out is None else [out]
    return pl.pallas_call(
        functools.partial(unpack_kernel, flips, panel),
        out_shape=shaped(2, 2, rows, 4 * width),
        in_specs=[
            *([pl.BlockSpec(memory_space=pltpu.VMEM)] * len(pairs)),
            *([pl.BlockSpec(memory_space=pl.ANY)] * len(given)),
        ],
        out_specs=pl.BlockSpec(memory_space=pl.ANY),
        scratch_shapes=[pltpu.VMEM((len(pairs), 2, rows, width), F32), pltpu.SemaphoreType.DMA((len(pairs),))],
        input_output_aliases={len(pairs): 0} if given else {},
        compiler_params=pltpu.CompilerParams(vmem_limit_bytes=8 * MIB),
        cost_estimate=pl.CostEstimate(flops=0, bytes_accessed=8 * sum(p.size for p in pairs), transcendentals=0),
    )(*pairs, *given)


def solution(mesh):
    def swap(value, axis, bit):
        return lax.ppermute(value, axis, [(i, i ^ bit) for i in range(mesh.shape[axis])])

    def all_but_last(value, axis, bit):
        while 2 * bit < mesh.shape[axis]:
            value = value + swap(value, axis, bit)
            bit *= 2
        return value, swap(value, axis, bit)

    def per_device(solved, upper_cols, coupling, inverse_diag, right_side):
        rows, cols = inverse_diag.shape[2:]
        n_rhs = right_side.shape[3]
        wide = n_rhs // 4

        def gather_matrix(block):
            got = swap(block, "row", NEAR)
            mine = jnp.concatenate([block, got], axis=1)
            beside = swap(mine, "col", SIDE)
            return (mine, beside, swap(mine, "row", CORE), swap(beside, "row", CORE))

        def chip_terms(panel):
            mine, send = prior(upper_cols, solved, panel, panel == 0)
            return mine, swap(send, "row", CORE), right_side[:, panel : panel + 1]

        def first_terms():
            shapes = [shaped(2, cols, wide), shaped(cols, wide), shaped(cols, wide)]
            given = chip_terms(0)
            beside, keep, send = call(split_kernel, given, shapes)
            beside = swap(beside, "col", SIDE)
            mine = keep + swap(send, "row", NEAR)
            keep, send = call(pack_kernel, (beside,), shapes[1:])
            return mine, keep + swap(send, "row", NEAR)

        def second_terms():
            given = chip_terms(1)
            keep, send = call(split_both_kernel, given, [shaped(2, cols, wide)] * 2)
            got = swap(send, "row", NEAR)
            keep, send = call(pick_kernel, (keep, got), [shaped(cols, wide)] * 2)
            return keep, swap(send, "col", SIDE)

        def apply_inverse(blocks, mine, got, flips):
            blocks = [block for flip in flips for block in blocks[2 * flip : 2 * flip + 2]]
            return call(
                functools.partial(inverse_kernel, flips),
                (*blocks, *mine, *got),
                [shaped(2 * len(flips) * rows, wide)],
                24 * MIB,
                24 * len(flips) * rows * cols * wide,
            )[0]

        def spread(own, others, partial=False):
            got = swap(others, "row", CORE)
            far = swap(jnp.concatenate([own[rows:], got[rows:]], axis=0), "row", NEAR)
            mine = [jnp.concatenate([own[:rows], got[:rows]], axis=0), far]
            if partial:
                mine = [sum(all_but_last(v, "col", 2 * SIDE)) for v in mine]
            return mine, [swap(v, "col", SIDE) for v in mine]

        inverse0 = gather_matrix(inverse_diag[:, 0])
        couple = gather_matrix(coupling)
        inverse1 = gather_matrix(inverse_diag[:, 1])

        pieces = [all_but_last(v, "row", 2 * NEAR) for v in first_terms()]
        part, got = all_but_last(apply_inverse(inverse0, *zip(*pieces), (0, 1)), "col", 2 * SIDE)
        keep1, beside1 = second_terms()
        mine, answer0 = call(
            couple_kernel,
            (*couple, part, got, keep1, beside1),
            [shaped(2 * cols, wide), shaped(4 * rows, wide)],
            24 * MIB,
            48 * rows * cols * wide,
        )
        mine0, other0 = spread(answer0[: 2 * rows], answer0[2 * rows :])
        mine, got = all_but_last(mine, "row", 2 * NEAR)
        others = apply_inverse(inverse1, (mine,), (got,), (1,))
        own = apply_inverse(inverse1, (mine,), (got,), (0,))
        out = unpack((*mine0, *other0), 0, (0, 1))
        mine1, other1 = spread(own, others, True)
        out = unpack(mine1, 1, (0,), out)
        return unpack(other1, 1, (1,), out)

    in_specs = (
        P(None, "row", None),
        P(None, None, "col", "row"),
        P(None, "col", "row"),
        P(None, None, "row", "col"),
        P(None, None, "col", None),
    )

    return jax.shard_map(
        per_device, mesh=mesh, in_specs=in_specs, out_specs=P(None, None, "row", None), check_vma=False
    )
```

```python
import functools

import jax
import jax.numpy as jnp
from jax import lax
from jax.experimental import pallas as pl
from jax.experimental.pallas import tpu as pltpu
from jax.sharding import PartitionSpec as P


CORE = 1
NEAR = 2
SIDE = 1
F32 = jnp.float32
BF16 = jnp.bfloat16
MIB = 1 << 20


def split(value):
    high = value.astype(BF16)
    return high, (value - high.astype(F32)).astype(BF16)


def dot(left, right):
    return jnp.dot(left, right, preferred_element_type=F32)


def product(left, right):
    (high, low), (both, right_high) = left, right
    width = right_high.shape[1]
    full = dot(high, both)
    return full[:, :width] + (full[:, width:] + dot(low, right_high))


def packed_right(value):
    high, low = split(value)
    return jnp.concatenate([high, low], axis=1), high


def lane_is_low(shape):
    return lax.broadcasted_iota(jnp.int32, shape, 1) < shape[1] // 2


def swap_halves(value):
    return pltpu.roll(value, value.shape[1] // 2, 1)


def complex_product(real, imag, right, conj):
    plain = product(split(real), right)
    cross = swap_halves(product(split(imag), right))
    low = lane_is_low(plain.shape)
    return plain + jnp.where(low if conj else jnp.logical_not(low), cross, -cross)


def place():
    row, col = lax.axis_index("row"), lax.axis_index("col")
    return row & 1, (row >> 1) & 1, col & 1, row >> 2, row, col


def call(kernel, arrays, outs, vmem=12 * MIB, flops=0):
    moved = sum(a.size * 4 for a in arrays) + sum(4 * o.size for o in outs)
    return pl.pallas_call(
        kernel,
        out_shape=outs,
        in_specs=[pl.BlockSpec(memory_space=pltpu.VMEM)] * len(arrays),
        out_specs=[pl.BlockSpec(memory_space=pltpu.VMEM)] * len(outs),
        compiler_params=pltpu.CompilerParams(vmem_limit_bytes=vmem),
        cost_estimate=pl.CostEstimate(flops=flops, bytes_accessed=moved, transcendentals=0),
    )(*arrays)


def shaped(*shape):
    return jax.ShapeDtypeStruct(shape, F32)


def multiply(left, right):
    (left_high, left_low), (right_high, right_low) = split(left), split(right)
    return dot(left_high, right_high) + (dot(left_high, right_low) + dot(left_low, right_high))


def prior_kernel(panel, chunks, upper, solved, keep_ref, send_ref, total, *scratch):
    step, width = solved.shape[1] // chunks, keep_ref.shape[2]
    spans = [pl.ds(i * step, step) for i in range(chunks)]
    copies = []
    if scratch:
        factor, value, factor_sems, value_sems = scratch
        for i, span in enumerate(spans):
            copies += [
                pltpu.make_async_copy(upper.at[:, pl.ds(panel, 1), :, span], factor.at[:, :, :, span], factor_sems.at[i]),
                pltpu.make_async_copy(solved.at[:, span], value.at[:, span], value_sems.at[i]),
            ]
        upper, solved, panel = factor, value, 0
    for copy in copies:
        copy.start()
    for i, span in enumerate(spans):
        for copy in copies[2 * i : 2 * i + 2]:
            copy.wait()
        left_real, left_imag = upper[0, panel, :, span], upper[1, panel, :, span]
        right_real, right_imag = solved[0, span], solved[1, span]
        first = multiply(left_real, right_real)
        second = multiply(left_imag, right_imag)
        mixed = multiply(left_real - left_imag, right_real + right_imag)
        real, imag = first + second, mixed - first + second
        total[0] = real if i == 0 else total[0] + real
        total[1] = imag if i == 0 else total[1] + imag
    low, high = total[:, :, :width], total[:, :, width:]
    core = place()[0]
    keep_ref[...] = jnp.where(core == 0, low, high)
    send_ref[...] = jnp.where(core == 0, high, low)


def prior(upper_cols, solved, panel, own_copies, chunks=4):
    cols, depth = upper_cols.shape[2:]
    width = solved.shape[2]
    scratch = [
        pltpu.VMEM((2, 1, cols, depth), F32),
        pltpu.VMEM((2, depth, width), F32),
        pltpu.SemaphoreType.DMA((chunks,)),
        pltpu.SemaphoreType.DMA((chunks,)),
    ]
    space = pl.ANY if own_copies else pltpu.VMEM
    return pl.pallas_call(
        functools.partial(prior_kernel, panel, chunks),
        out_shape=[shaped(2, cols, width // 2)] * 2,
        in_specs=[pl.BlockSpec(memory_space=space)] * 2,
        out_specs=[pl.BlockSpec(memory_space=pltpu.VMEM)] * 2,
        scratch_shapes=[pltpu.VMEM((2, cols, width), F32)] + (scratch if own_copies else []),
        compiler_params=pltpu.CompilerParams(vmem_limit_bytes=(52 if own_copies else 24) * MIB),
        cost_estimate=pl.CostEstimate(
            flops=18 * cols * depth * width, bytes_accessed=8 * (cols + width) * depth, transcendentals=0
        ),
    )(upper_cols, solved)


def pack(real, imag, near):
    low = lane_is_low(real.shape)
    first = jnp.where(low, real, swap_halves(imag))
    second = jnp.where(low, swap_halves(real), imag)
    return jnp.where(near == 0, first, second), jnp.where(near == 0, second, first)


def terms(ids, mine_ref, got_ref, right_ref):
    width = mine_ref.shape[2]
    right = right_ref[:, 0, :, pl.ds(pl.multiple_of(ids[0] * width, width), width)]
    return jnp.where((ids[1] == 0) & (ids[3] == 0), right, 0.0) - (mine_ref[...] + got_ref[...])


def split_kernel(mine_ref, got_ref, right_ref, beside_ref, keep_ref, send_ref):
    ids = place()
    value = terms(ids, mine_ref, got_ref, right_ref)
    width = beside_ref.shape[2]
    low, high = value[:, :, :width], value[:, :, width:]
    beside_ref[...] = jnp.where(ids[2] == 0, high, low)
    keep = jnp.where(ids[2] == 0, low, high)
    keep_ref[...], send_ref[...] = pack(keep[0], keep[1], ids[1])


def pack_kernel(value_ref, keep_ref, send_ref):
    ids = place()
    keep_ref[...], send_ref[...] = pack(value_ref[0], value_ref[1], ids[1])


def split_both_kernel(mine_ref, got_ref, right_ref, keep_ref, send_ref):
    ids = place()
    value = terms(ids, mine_ref, got_ref, right_ref)
    width = keep_ref.shape[2]
    for i in range(2):
        part = value[:, :, i * width : (i + 1) * width]
        keep_ref[i], send_ref[i] = pack(part[0], part[1], ids[1])


def pick_kernel(mine_ref, got_ref, keep_ref, send_ref):
    ids = place()
    first, second = mine_ref[0] + got_ref[0], mine_ref[1] + got_ref[1]
    keep_ref[...] = jnp.where(ids[2] == 0, first, second)
    send_ref[...] = jnp.where(ids[2] == 0, second, first)


def inverse_kernel(flips, *refs):
    ids = place()
    blocks, pieces, out_ref = refs[: 2 * len(flips)], refs[2 * len(flips) : -1], refs[-1]
    half = len(pieces) // 2
    rows, cols = blocks[0].shape[1] // 2, blocks[0].shape[2]
    value = jnp.concatenate([pieces[i][...] + pieces[half + i][...] for i in range(half)], axis=0)
    right = [packed_right(value[j * cols : (j + 1) * cols]) for j in range(2)]
    shape = (2 * rows, cols)
    row_place = lax.broadcasted_iota(jnp.int32, shape, 0)
    upper = row_place < rows
    row_place = row_place - jnp.where(upper, 0, rows)
    col_place = lax.broadcasted_iota(jnp.int32, shape, 1)
    for i, flip in enumerate(flips):
        row = ids[4] ^ (flip * CORE)
        row_id = row_place + jnp.where(upper, row, row ^ NEAR) * rows
        total = None
        for j, block in enumerate(blocks[2 * i : 2 * i + 2]):
            col_id = col_place + (ids[5] ^ (j * SIDE)) * cols
            inside = col_id <= row_id
            term = complex_product(
                jnp.where(inside, block[0], 0.0), jnp.where(inside, block[1], 0.0), right[j], False
            )
            total = term if total is None else total + term
        out_ref[pl.ds(i * 2 * rows, 2 * rows)] = total


def couple_kernel(a0, a1, a2, a3, mine_ref, got_ref, near_ref, far_ref, out_ref, answer_ref):
    cols, depth = near_ref.shape[0], 2 * a0.shape[2]
    answer = mine_ref[...] + got_ref[...]
    answer_ref[...] = answer
    right = [packed_right(answer[i * depth : (i + 1) * depth]) for i in range(2)]
    for j, base in enumerate((near_ref, far_ref)):
        value = base[...]
        for i, block in enumerate((a0, a2) if j == 0 else (a1, a3)):
            real, imag = (
                jnp.concatenate([block[part, pl.ds(near * cols, cols)] for near in range(2)], axis=1)
                for part in range(2)
            )
            value -= complex_product(real, imag, right[i], True)
        out_ref[pl.ds(j * cols, cols)] = value


def unpack_kernel(flips, panel, *refs):
    ids = place()
    out_ref, blocks, sem = refs[-3:]
    copies, at = [], 0
    for flip in flips:
        groups = []
        rows, width = blocks.shape[2:]
        while len(groups) < 4:
            groups += [refs[at].at[pl.ds(i, rows)] for i in range(0, refs[at].shape[0], rows)]
            at += 1
        for i in range(2):
            own, far = groups[i][...], groups[2 + i][...]
            low = lane_is_low(own.shape)
            start = pl.multiple_of(((ids[0] ^ i) * 2 + (ids[2] ^ flip)) * width, width)
            first = jnp.where(ids[1] == 0, own, far)
            second = jnp.where(ids[1] == 0, far, own)
            block = blocks.at[len(copies)]
            block[0] = jnp.where(low, first, swap_halves(second))
            block[1] = jnp.where(low, swap_halves(first), second)
            copies.append(
                pltpu.make_async_copy(block, out_ref.at[:, panel, :, pl.ds(start, width)], sem.at[len(copies)])
            )
            copies[-1].start()
    for copy in copies:
        copy.wait()


def unpack(pieces, panel, flips, out=None):
    rows, width = pieces[0].shape[0] // 2, pieces[0].shape[1]
    given = [] if out is None else [out]
    count = 2 * len(flips)
    return pl.pallas_call(
        functools.partial(unpack_kernel, flips, panel),
        out_shape=shaped(2, 2, rows, 4 * width),
        in_specs=[
            *([pl.BlockSpec(memory_space=pltpu.VMEM)] * len(pieces)),
            *([pl.BlockSpec(memory_space=pl.ANY)] * len(given)),
        ],
        out_specs=pl.BlockSpec(memory_space=pl.ANY),
        scratch_shapes=[pltpu.VMEM((count, 2, rows, width), F32), pltpu.SemaphoreType.DMA((count,))],
        input_output_aliases={len(pieces): 0} if given else {},
        compiler_params=pltpu.CompilerParams(vmem_limit_bytes=8 * MIB),
        cost_estimate=pl.CostEstimate(flops=0, bytes_accessed=8 * sum(p.size for p in pieces), transcendentals=0),
    )(*pieces, *given)


def solution(mesh):
    def swap(value, axis, bit):
        return lax.ppermute(value, axis, [(i, i ^ bit) for i in range(mesh.shape[axis])])

    def all_but_last(value, axis, bit):
        while 2 * bit < mesh.shape[axis]:
            value = value + swap(value, axis, bit)
            bit *= 2
        return value, swap(value, axis, bit)

    def per_device(solved, upper_cols, coupling, inverse_diag, right_side):
        rows, cols = inverse_diag.shape[2:]
        n_rhs = right_side.shape[3]
        wide = n_rhs // 4

        def gather_matrix(block):
            got = swap(block, "row", NEAR)
            mine = jnp.concatenate([block, got], axis=1)
            beside = swap(mine, "col", SIDE)
            return (mine, beside, swap(mine, "row", CORE), swap(beside, "row", CORE))

        def chip_terms(panel):
            mine, send = prior(upper_cols, solved, panel, panel == 0)
            return mine, swap(send, "row", CORE), right_side[:, panel : panel + 1]

        def first_terms():
            shapes = [shaped(2, cols, wide), shaped(cols, wide), shaped(cols, wide)]
            given = chip_terms(0)
            beside, keep, send = call(split_kernel, given, shapes)
            beside = swap(beside, "col", SIDE)
            mine = keep + swap(send, "row", NEAR)
            keep, send = call(pack_kernel, (beside,), shapes[1:])
            return mine, keep + swap(send, "row", NEAR)

        def second_terms():
            given = chip_terms(1)
            keep, send = call(split_both_kernel, given, [shaped(2, cols, wide)] * 2)
            got = swap(send, "row", NEAR)
            keep, send = call(pick_kernel, (keep, got), [shaped(cols, wide)] * 2)
            return keep, swap(send, "col", SIDE)

        def apply_inverse(blocks, mine, got, flips):
            blocks = [block for flip in flips for block in blocks[2 * flip : 2 * flip + 2]]
            return call(
                functools.partial(inverse_kernel, flips),
                (*blocks, *mine, *got),
                [shaped(2 * len(flips) * rows, wide)],
                24 * MIB,
                24 * len(flips) * rows * cols * wide,
            )[0]

        def spread(own, others, partial=False):
            got = swap(others, "row", CORE)
            mine = [jnp.concatenate([own[:rows], got[:rows]], axis=0)]
            if partial:
                mine += [swap(v[rows:], "row", NEAR) for v in (own, got)]
                mine = [sum(all_but_last(v, "col", 2 * SIDE)) for v in mine]
            else:
                mine.append(swap(jnp.concatenate([own[rows:], got[rows:]], axis=0), "row", NEAR))
            return mine, [swap(v, "col", SIDE) for v in mine]

        inverse0 = gather_matrix(inverse_diag[:, 0])
        couple = gather_matrix(coupling)
        inverse1 = gather_matrix(inverse_diag[:, 1])

        pieces = [all_but_last(v, "row", 2 * NEAR) for v in first_terms()]
        part, got = all_but_last(apply_inverse(inverse0, *zip(*pieces), (0, 1)), "col", 2 * SIDE)
        keep1, beside1 = second_terms()
        mine, answer0 = call(
            couple_kernel,
            (*couple, part, got, keep1, beside1),
            [shaped(2 * cols, wide), shaped(4 * rows, wide)],
            24 * MIB,
            48 * rows * cols * wide,
        )
        mine0, other0 = spread(answer0[: 2 * rows], answer0[2 * rows :])
        mine, got = all_but_last(mine, "row", 2 * NEAR)
        others = apply_inverse(inverse1, (mine,), (got,), (1,))
        own = apply_inverse(inverse1, (mine,), (got,), (0,))
        out = unpack((*mine0, *other0), 0, (0, 1))
        mine1, other1 = spread(own, others, True)
        out = unpack(mine1, 1, (0,), out)
        return unpack(other1, 1, (1,), out)

    in_specs = (
        P(None, "row", None),
        P(None, None, "col", "row"),
        P(None, "col", "row"),
        P(None, None, "row", "col"),
        P(None, None, "col", None),
    )

    return jax.shard_map(
        per_device, mesh=mesh, in_specs=in_specs, out_specs=P(None, None, "row", None), check_vma=False
    )
```

```python
import functools

import jax
import jax.numpy as jnp
from jax import lax
from jax.experimental import pallas as pl
from jax.experimental.pallas import tpu as pltpu
from jax.sharding import PartitionSpec as P


CORE = 1
NEAR = 2
SIDE = 1
F32 = jnp.float32
BF16 = jnp.bfloat16
MIB = 1 << 20


def split(value):
    high = value.astype(BF16)
    return high, (value - high.astype(F32)).astype(BF16)


def dot(left, right):
    return jnp.dot(left, right, preferred_element_type=F32)


def product(left, right):
    (high, low), (both, right_high) = left, right
    width = right_high.shape[1]
    full = dot(high, both)
    return full[:, :width] + (full[:, width:] + dot(low, right_high))


def packed_right(value):
    high, low = split(value)
    return jnp.concatenate([high, low], axis=1), high


def lane_is_low(shape):
    return lax.broadcasted_iota(jnp.int32, shape, 1) < shape[1] // 2


def swap_halves(value):
    return pltpu.roll(value, value.shape[1] // 2, 1)


def complex_product(real, imag, right, conj):
    plain = product(split(real), right)
    cross = swap_halves(product(split(imag), right))
    low = lane_is_low(plain.shape)
    return plain + jnp.where(low if conj else jnp.logical_not(low), cross, -cross)


def place():
    row, col = lax.axis_index("row"), lax.axis_index("col")
    return row & 1, (row >> 1) & 1, col & 1, row >> 2, row, col


def call(kernel, arrays, outs, vmem=12 * MIB, flops=0):
    moved = sum(a.size * 4 for a in arrays) + sum(4 * o.size for o in outs)
    return pl.pallas_call(
        kernel,
        out_shape=outs,
        in_specs=[pl.BlockSpec(memory_space=pltpu.VMEM)] * len(arrays),
        out_specs=[pl.BlockSpec(memory_space=pltpu.VMEM)] * len(outs),
        compiler_params=pltpu.CompilerParams(vmem_limit_bytes=vmem),
        cost_estimate=pl.CostEstimate(flops=flops, bytes_accessed=moved, transcendentals=0),
    )(*arrays)


def shaped(*shape):
    return jax.ShapeDtypeStruct(shape, F32)


def multiply(left, right):
    (left_high, left_low), (right_high, right_low) = split(left), split(right)
    return dot(left_high, right_high) + (dot(left_high, right_low) + dot(left_low, right_high))


def prior_kernel(panel, chunks, upper, solved, keep_ref, send_ref, total, *scratch):
    step, width = solved.shape[1] // chunks, keep_ref.shape[2]
    spans = [pl.ds(i * step, step) for i in range(chunks)]
    copies = []
    if scratch:
        factor, value, factor_sems, value_sems = scratch
        for i, span in enumerate(spans):
            copies += [
                pltpu.make_async_copy(upper.at[:, pl.ds(panel, 1), :, span], factor.at[:, :, :, span], factor_sems.at[i]),
                pltpu.make_async_copy(solved.at[:, span], value.at[:, span], value_sems.at[i]),
            ]
        upper, solved, panel = factor, value, 0
    for copy in copies:
        copy.start()
    for i, span in enumerate(spans):
        for copy in copies[2 * i : 2 * i + 2]:
            copy.wait()
        left_real, left_imag = upper[0, panel, :, span], upper[1, panel, :, span]
        right_real, right_imag = solved[0, span], solved[1, span]
        first = multiply(left_real, right_real)
        second = multiply(left_imag, right_imag)
        mixed = multiply(left_real - left_imag, right_real + right_imag)
        real, imag = first + second, mixed - first + second
        total[0] = real if i == 0 else total[0] + real
        total[1] = imag if i == 0 else total[1] + imag
    low, high = total[:, :, :width], total[:, :, width:]
    core = place()[0]
    keep_ref[...] = jnp.where(core == 0, low, high)
    send_ref[...] = jnp.where(core == 0, high, low)


def prior(upper_cols, solved, panel, own_copies, chunks=4):
    cols, depth = upper_cols.shape[2:]
    width = solved.shape[2]
    scratch = [
        pltpu.VMEM((2, 1, cols, depth), F32),
        pltpu.VMEM((2, depth, width), F32),
        pltpu.SemaphoreType.DMA((chunks,)),
        pltpu.SemaphoreType.DMA((chunks,)),
    ]
    space = pl.ANY if own_copies else pltpu.VMEM
    return pl.pallas_call(
        functools.partial(prior_kernel, panel, chunks),
        out_shape=[shaped(2, cols, width // 2)] * 2,
        in_specs=[pl.BlockSpec(memory_space=space)] * 2,
        out_specs=[pl.BlockSpec(memory_space=pltpu.VMEM)] * 2,
        scratch_shapes=[pltpu.VMEM((2, cols, width), F32)] + (scratch if own_copies else []),
        compiler_params=pltpu.CompilerParams(vmem_limit_bytes=(52 if own_copies else 24) * MIB),
        cost_estimate=pl.CostEstimate(
            flops=18 * cols * depth * width, bytes_accessed=8 * (cols + width) * depth, transcendentals=0
        ),
    )(upper_cols, solved)


def pack(real, imag, near):
    low = lane_is_low(real.shape)
    first = jnp.where(low, real, swap_halves(imag))
    second = jnp.where(low, swap_halves(real), imag)
    return jnp.where(near == 0, first, second), jnp.where(near == 0, second, first)


def terms(ids, mine_ref, got_ref, right_ref):
    width = mine_ref.shape[2]
    right = right_ref[:, 0, :, pl.ds(pl.multiple_of(ids[0] * width, width), width)]
    return jnp.where((ids[1] == 0) & (ids[3] == 0), right, 0.0) - (mine_ref[...] + got_ref[...])


def split_kernel(mine_ref, got_ref, right_ref, beside_ref, keep_ref, send_ref):
    ids = place()
    value = terms(ids, mine_ref, got_ref, right_ref)
    width = beside_ref.shape[2]
    low, high = value[:, :, :width], value[:, :, width:]
    beside_ref[...] = jnp.where(ids[2] == 0, high, low)
    keep = jnp.where(ids[2] == 0, low, high)
    keep_ref[...], send_ref[...] = pack(keep[0], keep[1], ids[1])


def pack_kernel(value_ref, keep_ref, send_ref):
    ids = place()
    keep_ref[...], send_ref[...] = pack(value_ref[0], value_ref[1], ids[1])


def split_both_kernel(mine_ref, got_ref, right_ref, keep_ref, send_ref):
    ids = place()
    value = terms(ids, mine_ref, got_ref, right_ref)
    width = keep_ref.shape[2]
    for i in range(2):
        part = value[:, :, i * width : (i + 1) * width]
        keep_ref[i], send_ref[i] = pack(part[0], part[1], ids[1])


def pick_kernel(mine_ref, got_ref, keep_ref, send_ref):
    ids = place()
    first, second = mine_ref[0] + got_ref[0], mine_ref[1] + got_ref[1]
    keep_ref[...] = jnp.where(ids[2] == 0, first, second)
    send_ref[...] = jnp.where(ids[2] == 0, second, first)


def inverse_kernel(flips, *refs):
    ids = place()
    blocks, pieces, out_ref = refs[: 2 * len(flips)], refs[2 * len(flips) : -1], refs[-1]
    half = len(pieces) // 2
    rows, cols = blocks[0].shape[1] // 2, blocks[0].shape[2]
    value = jnp.concatenate([pieces[i][...] + pieces[half + i][...] for i in range(half)], axis=0)
    right = [packed_right(value[j * cols : (j + 1) * cols]) for j in range(2)]
    shape = (2 * rows, cols)
    row_place = lax.broadcasted_iota(jnp.int32, shape, 0)
    upper = row_place < rows
    row_place = row_place - jnp.where(upper, 0, rows)
    col_place = lax.broadcasted_iota(jnp.int32, shape, 1)
    for i, flip in enumerate(flips):
        row = ids[4] ^ (flip * CORE)
        row_id = row_place + jnp.where(upper, row, row ^ NEAR) * rows
        total = None
        for j, block in enumerate(blocks[2 * i : 2 * i + 2]):
            col_id = col_place + (ids[5] ^ (j * SIDE)) * cols
            inside = col_id <= row_id
            term = complex_product(
                jnp.where(inside, block[0], 0.0), jnp.where(inside, block[1], 0.0), right[j], False
            )
            total = term if total is None else total + term
        out_ref[pl.ds(i * 2 * rows, 2 * rows)] = total


def couple_kernel(first_ref, second_ref, *refs):
    complete = len(refs) == 5
    *given, base_ref, out_ref = refs[:4] if complete else refs
    answer = given[0][...]
    if complete:
        answer = answer + given[1][...]
        refs[4][...] = answer
    cols, depth = base_ref.shape[0], 2 * first_ref.shape[2]
    value = base_ref[...]
    for i, block in enumerate((first_ref, second_ref)):
        real, imag = (
            jnp.concatenate([block[part, pl.ds(near * cols, cols)] for near in range(2)], axis=1) for part in range(2)
        )
        value -= complex_product(real, imag, packed_right(answer[i * depth : (i + 1) * depth]), True)
    out_ref[...] = value


def unpack_kernel(flips, panel, *refs):
    ids = place()
    out_ref, blocks, sem = refs[-3:]
    copies, at = [], 0
    for flip in flips:
        groups = []
        rows, width = blocks.shape[2:]
        while len(groups) < 4:
            groups += [refs[at].at[pl.ds(i, rows)] for i in range(0, refs[at].shape[0], rows)]
            at += 1
        for i in range(2):
            own, far = groups[i][...], groups[2 + i][...]
            low = lane_is_low(own.shape)
            start = pl.multiple_of(((ids[0] ^ i) * 2 + (ids[2] ^ flip)) * width, width)
            first = jnp.where(ids[1] == 0, own, far)
            second = jnp.where(ids[1] == 0, far, own)
            block = blocks.at[len(copies)]
            block[0] = jnp.where(low, first, swap_halves(second))
            block[1] = jnp.where(low, swap_halves(first), second)
            copies.append(
                pltpu.make_async_copy(block, out_ref.at[:, panel, :, pl.ds(start, width)], sem.at[len(copies)])
            )
            copies[-1].start()
    for copy in copies:
        copy.wait()


def unpack(pieces, panel, flips, out=None):
    rows, width = pieces[0].shape[0] // 2, pieces[0].shape[1]
    given = [] if out is None else [out]
    count = 2 * len(flips)
    return pl.pallas_call(
        functools.partial(unpack_kernel, flips, panel),
        out_shape=shaped(2, 2, rows, 4 * width),
        in_specs=[
            *([pl.BlockSpec(memory_space=pltpu.VMEM)] * len(pieces)),
            *([pl.BlockSpec(memory_space=pl.ANY)] * len(given)),
        ],
        out_specs=pl.BlockSpec(memory_space=pl.ANY),
        scratch_shapes=[pltpu.VMEM((count, 2, rows, width), F32), pltpu.SemaphoreType.DMA((count,))],
        input_output_aliases={len(pieces): 0} if given else {},
        compiler_params=pltpu.CompilerParams(vmem_limit_bytes=8 * MIB),
        cost_estimate=pl.CostEstimate(flops=0, bytes_accessed=8 * sum(p.size for p in pieces), transcendentals=0),
    )(*pieces, *given)


def solution(mesh):
    def swap(value, axis, bit):
        return lax.ppermute(value, axis, [(i, i ^ bit) for i in range(mesh.shape[axis])])

    def all_but_last(value, axis, bit):
        while 2 * bit < mesh.shape[axis]:
            value = value + swap(value, axis, bit)
            bit *= 2
        return value, swap(value, axis, bit)

    def per_device(solved, upper_cols, coupling, inverse_diag, right_side):
        rows, cols = inverse_diag.shape[2:]
        n_rhs = right_side.shape[3]
        wide = n_rhs // 4

        def gather_matrix(block):
            got = swap(block, "row", NEAR)
            mine = jnp.concatenate([block, got], axis=1)
            beside = swap(mine, "col", SIDE)
            return (mine, beside, swap(mine, "row", CORE), swap(beside, "row", CORE))

        def chip_terms(panel):
            mine, send = prior(upper_cols, solved, panel, panel == 0)
            return mine, swap(send, "row", CORE), right_side[:, panel : panel + 1]

        def first_terms():
            shapes = [shaped(2, cols, wide), shaped(cols, wide), shaped(cols, wide)]
            given = chip_terms(0)
            beside, keep, send = call(split_kernel, given, shapes)
            beside = swap(beside, "col", SIDE)
            mine = keep + swap(send, "row", NEAR)
            keep, send = call(pack_kernel, (beside,), shapes[1:])
            return mine, keep + swap(send, "row", NEAR)

        def second_terms():
            given = chip_terms(1)
            keep, send = call(split_both_kernel, given, [shaped(2, cols, wide)] * 2)
            got = swap(send, "row", NEAR)
            keep, send = call(pick_kernel, (keep, got), [shaped(cols, wide)] * 2)
            return keep, swap(send, "col", SIDE)

        def apply_inverse(blocks, mine, got, flips):
            blocks = [block for flip in flips for block in blocks[2 * flip : 2 * flip + 2]]
            return call(
                functools.partial(inverse_kernel, flips),
                (*blocks, *mine, *got),
                [shaped(2 * len(flips) * rows, wide)],
                24 * MIB,
                24 * len(flips) * rows * cols * wide,
            )[0]

        def spread(own, others, partial=False):
            got = swap(others, "row", CORE)
            mine = [jnp.concatenate([own[:rows], got[:rows]], axis=0)]
            if partial:
                mine += [swap(v[rows:], "row", NEAR) for v in (own, got)]
                mine = [sum(all_but_last(v, "col", 2 * SIDE)) for v in mine]
            else:
                mine.append(swap(jnp.concatenate([own[rows:], got[rows:]], axis=0), "row", NEAR))
            return mine, [swap(v, "col", SIDE) for v in mine]

        inverse0 = gather_matrix(inverse_diag[:, 0])
        couple = gather_matrix(coupling)
        inverse1 = gather_matrix(inverse_diag[:, 1])

        pieces = [all_but_last(v, "row", 2 * NEAR) for v in first_terms()]
        part, got = all_but_last(apply_inverse(inverse0, *zip(*pieces), (0, 1)), "col", 2 * SIDE)
        keep1, beside1 = second_terms()
        flops = 24 * rows * cols * wide
        mine, answer0 = call(
            couple_kernel,
            (couple[0], couple[2], part, got, keep1),
            [shaped(cols, wide), shaped(4 * rows, wide)],
            24 * MIB,
            flops,
        )
        (other,) = call(couple_kernel, (couple[1], couple[3], answer0, beside1), [shaped(cols, wide)], 24 * MIB, flops)
        mine0, other0 = spread(answer0[: 2 * rows], answer0[2 * rows :])
        pieces = [*zip(*(all_but_last(v, "row", 2 * NEAR) for v in (mine, other)))]
        others = apply_inverse(inverse1, *pieces, (1,))
        own = apply_inverse(inverse1, *pieces, (0,))
        out = unpack((*mine0, *other0), 0, (0, 1))
        mine1, other1 = spread(own, others, True)
        out = unpack(mine1, 1, (0,), out)
        return unpack(other1, 1, (1,), out)

    in_specs = (
        P(None, "row", None),
        P(None, None, "col", "row"),
        P(None, "col", "row"),
        P(None, None, "row", "col"),
        P(None, None, "col", None),
    )

    return jax.shard_map(
        per_device, mesh=mesh, in_specs=in_specs, out_specs=P(None, None, "row", None), check_vma=False
    )
```
